32 devices in a mesh: feat: 8 (over z, core), node: 4 (over y, x).
Axes of the slice: x: 2, y: 2, z: 4, core: 2. Of those that a mesh axis runs over, the one named last changes fastest.
Arguments:
- node_features: bfloat16 [1024, 4, 1024], P('feat', 'node'), may hold values from -6 to 6
- weight: bfloat16 [1024, 256], P('feat'), may hold values from -0.1875 to 0.1875
- out_bias: float32 [256], replicated, may hold values from -3 to 3
- edge_tiles: bfloat16 [4, 8, 8, 128, 128], P('node', 'feat'), may hold values from 0.049804688 to 1
- tile_column: int32 [4, 8, 8], P('node', 'feat'), may hold values from 0 to 7, as said below
- tile_count: int32 [4, 8], P('node', 'feat'), may hold values from 1 to 8, as said below
- grad_hidden: bfloat16 [4, 1024, 256], P('node', 'feat'), may hold values from -6 to 6
Outputs:
- hidden: bfloat16 [4, 1024, 256], P('node', 'feat')
- grad_features: bfloat16 [1024, 4, 1024], P('feat', 'node')
- weight_grad: float32 [1024, 256], P('feat')
The draws below stay inside these ranges and needn't reach their ends.
Inputs may be any that keep to these rules, and one draw needn't show every extreme that they name: `tile_column`: the 8 column blocks listed for one row block are distinct, live slots or not. `tile_count`: slots of a row block beyond its count are ignored. In every cluster some row block has exactly 8 live tiles.
All inputs are finite; a program needn't handle non-finite values.
Results may differ from the reference program's by a relative error of at most 0.007.
Values may be sent and summed in bfloat16 or wider, within the bound.
A program may use at most 64 MiB of HBM per device.

```python
import math
import jax
import jax.numpy as jnp
from jax import lax

F = 1024
H = 256
TILE = 128
TPR = 8
NBLK = 8
R = 1024
CLUSTERS = 4
NODES = 4096


def draw_tile_column(key, part):
    row_keys = jax.random.split(key, CLUSTERS * NBLK)

    def one_row(row_key):
        return jax.random.permutation(row_key, NBLK)[:TPR].astype(jnp.int32)
    picked = jax.vmap(one_row)(row_keys)
    return picked.reshape(CLUSTERS, NBLK, TPR)


def draw_tile_count(key, part):
    key_one, key_two, key_three = jax.random.split(key, 3)
    grid_shape = (CLUSTERS, NBLK)
    largest = jnp.maximum(jax.random.randint(key_one, grid_shape, 1, TPR + 1), jax.random.randint(key_two, grid_shape, 1, TPR + 1))
    busiest = jax.random.randint(key_three, (CLUSTERS, 1), 0, NBLK)
    block_ids = jnp.arange(NBLK, dtype=jnp.int32)[None, :]
    return jnp.where(block_ids == busiest, TPR, largest).astype(jnp.int32)


def block_scale(stream_key, dims, cuts, least, top_value):
    def one(axis_at, shards_of):
        heights = jax.random.uniform(jax.random.fold_in(jax.random.fold_in(stream_key, 6), axis_at), (shards_of,), jnp.float32, least / len(cuts), top_value / len(cuts))
        return jnp.repeat(jnp.exp(heights), dims[axis_at] // shards_of).reshape((-1,) + (1,) * (len(dims) - axis_at - 1))

    level = one(*cuts[0])
    for cut in cuts[1:]:
        level = level * one(*cut)
    return level


def centred(key, dims, width, reach, shards=(), kind=jnp.bfloat16):
    drawn = jax.random.normal(key, dims, jnp.float32) * width
    if len(shards) > 0:
        drawn = block_scale(key, dims, shards, -0.22, 0.18) * drawn
    return jnp.clip(drawn, min=-reach, max=reach).astype(kind)


def setup_inputs(seed: int = 0) -> dict:
    seeds = jax.random.split(jax.random.key(seed), 8)
    node_features = centred(seeds[0], (F, CLUSTERS, R), 1.0, 6.0, ((0, 8), (1, 4)))
    weight = centred(seeds[1], (F, H), F ** -0.5, 0.1875, ((0, 8),))
    out_bias = centred(seeds[2], (H,), 0.5, 3.0, (), jnp.float32)
    edge_tiles = jnp.clip(jnp.exp(math.log(1.0) - 2.9996462 * jax.random.uniform(seeds[3], (CLUSTERS, NBLK, TPR, TILE, TILE), jnp.float32) ** block_scale(seeds[3], (CLUSTERS, NBLK, TPR, TILE, TILE), ((0, 4), (1, 8)), -0.2, 0.2)), 0.049804688, 1.0).astype(jnp.bfloat16)
    tile_column = draw_tile_column(jax.random.fold_in(seeds[7], 71), 0)
    tile_count = draw_tile_count(jax.random.fold_in(seeds[7], 71), 0)
    grad_hidden = centred(seeds[6], (CLUSTERS, R, H), 1.0, 6.0, ((0, 4), (1, 8)))
    return {"node_features": node_features, "weight": weight, "out_bias": out_bias, "edge_tiles": edge_tiles, "tile_column": tile_column, "tile_count": tile_count, "grad_hidden": grad_hidden}


def gelu_tanh(pre_value):
    return jax.nn.gelu(pre_value, approximate=True)

def one_cluster(weight, out_bias, cluster_feats, cluster_tiles, cluster_cols, cluster_count, cluster_grad):
    slot_ids = jnp.arange(TPR, dtype=jnp.int32)
    projected = lax.dot_general(cluster_feats, weight, (((0,), (0,)), ((), ())), preferred_element_type=jnp.float32).astype(jnp.bfloat16)
    block_rows = projected.reshape(NBLK, TILE, H)
    live_mask = (slot_ids[None, :] < cluster_count[:, None]).astype(jnp.bfloat16)
    masked = cluster_tiles * live_mask[:, :, None, None]
    masked_wide = masked.astype(jnp.float32)
    degree = lax.optimization_barrier(jnp.sum(masked_wide, axis=(1, 3)))
    chosen = block_rows[cluster_cols]
    summed = jnp.einsum('bsij,bsjh->bih', masked_wide, chosen.astype(jnp.float32))
    row_scale = lax.rsqrt(degree)[:, :, None]
    pre_act = summed * row_scale + out_bias
    activated, backward = jax.vjp(gelu_tanh, pre_act)
    grad_pre, = backward(cluster_grad.reshape(NBLK, TILE, H).astype(jnp.float32))
    scaled = (grad_pre * row_scale).astype(jnp.bfloat16)
    tile_terms = jnp.einsum('bsij,bih->bsjh', masked_wide, scaled.astype(jnp.float32)).astype(jnp.bfloat16)
    grad_proj = jnp.zeros((NBLK, TILE, H), jnp.float32).at[cluster_cols].add(tile_terms.astype(jnp.float32))
    grad_rounded = grad_proj.astype(jnp.bfloat16).reshape(NBLK * TILE, H)
    grad_feat = lax.dot_general(weight, grad_rounded, (((1,), (1,)), ((), ())), preferred_element_type=jnp.float32).astype(jnp.bfloat16)
    grad_weight = lax.dot_general(cluster_feats, grad_rounded, (((1,), (0,)), ((), ())), preferred_element_type=jnp.float32)
    return (activated.astype(jnp.bfloat16).reshape(NBLK * TILE, H), grad_feat, grad_weight)

def reference(node_features, weight, out_bias, edge_tiles, tile_column, tile_count, grad_hidden):
    per_cluster = (jnp.moveaxis(node_features, 1, 0), edge_tiles, tile_column, tile_count, grad_hidden)

    def step_one(running, pieces):
        cluster_feats, cluster_tiles, cluster_cols, cluster_count, cluster_grad = pieces
        activated, grad_feat, grad_weight = one_cluster(weight, out_bias, cluster_feats, cluster_tiles, cluster_cols, cluster_count, cluster_grad)
        return (running + grad_weight, (activated, grad_feat))
    start_grad = jnp.zeros((F, H), jnp.float32)
    total_grad, (hidden, grad_cols) = lax.scan(step_one, start_grad, per_cluster)
    grad_features = jnp.moveaxis(grad_cols, 0, 1)
    weight_grad = total_grad * (1.0 / math.sqrt(NODES))
    return (hidden, grad_features, weight_grad)
```

```python
import functools
import math

import jax
import jax.numpy as jnp
from jax import lax
from jax.experimental import pallas as pl
from jax.experimental.pallas import tpu as pltpu
from jax.sharding import PartitionSpec as P

MESH = pl.DeviceIdType.MESH
F32 = jnp.float32
BF16 = jnp.bfloat16
CHUNKS = 2
ROOT = math.sqrt(2.0 / math.pi)


def flip(index, bit):
    return index + bit * (1 - 2 * ((index // bit) % 2))


def flip_many(index, mask, steps):
    for j in range(steps):
        if (mask >> j) & 1:
            index = flip(index, 1 << j)
    return index


def tn(a, b):
    return lax.dot_general(a, b, (((0,), (0,)), ((), ())), preferred_element_type=F32)


def nt(a, b):
    return lax.dot_general(a, b, (((1,), (1,)), ((), ())), preferred_element_type=F32)


def nn(a, b):
    return lax.dot_general(a, b, (((1,), (0,)), ((), ())), preferred_element_type=F32)


def kernel(sizes, cols, count, feats, weight, bias, tiles, grad_hidden,
           hidden, grad_feat, weight_grad,
           x_send, x_pair, w_pair, a_send, a_pair,
           rs_out, rs_in, gath, part_out, part_in, sc_pair, rt_out, rt_in, ggath, gfwd,
           wg_out, wg_in,
           ex_s, ex_r, rs_s, rs_r, ag_s, ag_r, p_s, p_r, s_s, s_r, rt_s, rt_r,
           gg_s, gg_r, fw_s, fw_r, wg_s, wg_r):
    zs, nodes, slots, tr, fd, hw, total = sizes
    zbits, nbits = zs.bit_length() - 1, nodes.bit_length() - 1
    hc = hw // CHUNKS
    feat_at = lax.axis_index("feat")
    node_at = lax.axis_index("node")
    core = feat_at % 2
    z = feat_at // 2
    mate = {"feat": z * 2 + 1 - core}

    def z_peer(j):
        return {"feat": flip(z, 1 << j) * 2 + core}

    def n_peer(j):
        return {"node": flip(node_at, 1 << j)}

    def push(src, dst, ss, rr, dev):
        copy = pltpu.make_async_remote_copy(
            src_ref=src, dst_ref=dst, send_sem=ss, recv_sem=rr,
            device_id=dev, device_id_type=MESH)
        copy.start()
        sent.append(copy)
        return copy

    sent = []
    barrier = pltpu.get_barrier_semaphore()
    peers = [mate] + [z_peer(j) for j in range(zbits)] + [n_peer(j) for j in range(nbits)]
    for dev in peers:
        pl.semaphore_signal(barrier, inc=1, device_id=dev, device_id_type=MESH)

    zrel = [flip_many(z, r, zbits) for r in range(zs)]

    def rows_of(r, parity):
        return pl.multiple_of((zrel[r] * 2 + parity) * tr, tr)

    for r in range(zs):
        x_pair[r, 0:fd, :] = feats[:, pl.ds(rows_of(r, core), tr)]
        x_send[r] = feats[:, pl.ds(rows_of(r, 1 - core), tr)]
    w_pair[0:fd, :] = weight[...]
    pl.semaphore_wait(barrier, len(peers))
    ex_x = push(x_send, x_pair.at[:, pl.ds(fd, fd), :], ex_s.at[0], ex_r.at[0], mate)
    ex_w = push(weight, w_pair.at[pl.ds(fd, fd)], ex_s.at[1], ex_r.at[1], mate)

    degree = jnp.zeros((tr, 1), F32)
    live = count[0]

    def listed(block):
        where = jnp.int32(0)
        alive = jnp.int32(0)
        for s in range(slots):
            hit = cols[s] == block
            where = jnp.where(hit, s, where)
            alive = jnp.where(hit, jnp.where(s < live, 1, 0), alive)
        return tiles[where].astype(F32) * alive.astype(F32)

    for r in range(zs):
        other = listed(zrel[r] * 2 + 1 - core)
        a_send[:, r * tr:(r + 1) * tr] = other.astype(BF16)
        mine = listed(zrel[r] * 2 + core)
        a_pair[0:tr, r * tr:(r + 1) * tr] = mine.astype(BF16)
        degree = degree + jnp.sum(mine + other, axis=1, keepdims=True)
    ex_a = push(a_send, a_pair.at[pl.ds(tr, tr)], ex_s.at[2], ex_r.at[2], mate)
    row_scale = lax.rsqrt(degree)
    ex_x.wait_recv()
    ex_w.wait_recv()

    def hs(k):
        return slice(k * hc, (k + 1) * hc)

    def slot_of(j):
        return sum(zs >> (i + 1) for i in range(j))

    def rs_first(k, make, out, into, ss, rr):
        kept = {}
        n = zs // 2
        for m in range(n):
            out[k, m] = make(1 + 2 * m).astype(BF16)
        copies = [push(out.at[k, pl.ds(0, n)], into.at[k, pl.ds(0, n)],
                       ss.at[k, 0], rr.at[k, 0], z_peer(0))]
        for m in range(n):
            kept[2 * m] = make(2 * m)
        return kept, copies[0]

    def rs_next(k, j, kept, copy, out, into, ss, rr):
        base = slot_of(j - 1)
        copy.wait_recv()
        step = 1 << j
        held = {}
        for m in range(zs >> j):
            held[m * step] = kept[m * step] + into[k, base + m].astype(F32)
        if j == zbits:
            return held[0]
        n = zs >> (j + 1)
        at = slot_of(j)
        for m in range(n):
            out[k, at + m] = held[step + 2 * step * m].astype(BF16)
        nxt = push(out.at[k, pl.ds(at, n)], into.at[k, pl.ds(at, n)],
                   ss.at[k, j], rr.at[k, j], z_peer(j))
        return {2 * step * m: held[2 * step * m] for m in range(n)}, nxt

    def gather_send(k, r, low, buf, ss, rr, waits):
        for j in reversed(range(low)):
            slot = r + (1 << j)
            waits[slot] = push(buf.at[k, r], buf.at[k, slot], ss.at[k, slot],
                               rr.at[k, slot], z_peer(j))

    ks = range(CHUNKS)

    def reduce_scatter(make, out, into, ss, rr):
        state = [rs_first(k, functools.partial(make, k), out, into, ss, rr) for k in ks]
        for j in range(1, zbits):
            state = [rs_next(k, j, *state[k], out, into, ss, rr) for k in ks]
        return state

    def gather(k_waits, k, j, buf, ss, rr, seen):
        step = 1 << (j + 1)
        for m in range(zs // step):
            slot = m * step + (1 << j)
            k_waits[slot].wait_recv()
            gather_send(k, slot, j, buf, ss, rr, k_waits)
            seen(k, slot)

    def project(k, r):
        return tn(x_pair[r], w_pair[:, hs(k)])

    state = reduce_scatter(project, rs_out, rs_in, rs_s, rs_r)
    waits = [dict() for _ in ks]
    for k in ks:
        own = rs_next(k, zbits, *state[k], rs_out, rs_in, rs_s, rs_r)
        gath[k, 0] = own.astype(BF16)
        gather_send(k, 0, zbits, gath, ag_s, ag_r, waits[k])
    for j in reversed(range(1, zbits)):
        for k in ks:
            gather(waits[k], k, j, gath, ag_s, ag_r, lambda k, r: None)
    ex_a.wait_recv()
    mine_sum, parts = [], []
    for k in ks:
        gather(waits[k], k, 0, gath, ag_s, ag_r, lambda k, r: None)
        both = nn(a_pair[...], gath[k].reshape(zs * tr, hc))
        part_out[k] = both[tr:]
        parts.append(push(part_out.at[k], part_in.at[k], p_s.at[k], p_r.at[k], mate))
        mine_sum.append(both[:tr])
    scs = []
    for k in ks:
        parts[k].wait_recv()
        v = (mine_sum[k] + part_in[k]) * row_scale + bias[:, hs(k)]
        v2 = v * v
        t = jnp.tanh(ROOT * (v + 0.044715 * v2 * v))
        hidden[:, hs(k)] = (0.5 * v * (1.0 + t)).astype(BF16)
        slope = 0.5 * (1.0 + t) + 0.5 * v * (1.0 - t * t) * (ROOT * (1.0 + 3 * 0.044715 * v2))
        grad_pre = grad_hidden[:, hs(k)].astype(F32) * slope
        sc_pair[k, 0:tr] = (grad_pre * row_scale).astype(BF16)
        scs.append(push(sc_pair.at[k, pl.ds(0, tr)], sc_pair.at[k, pl.ds(tr, tr)],
                        s_s.at[k], s_r.at[k], mate))

    def terms(k, r):
        if r == 1:
            scs[k].wait_recv()
        return tn(a_pair[:, r * tr:(r + 1) * tr], sc_pair[k])

    state = reduce_scatter(terms, rt_out, rt_in, rt_s, rt_r)
    waits = [dict() for _ in ks]
    fwd = [dict() for _ in ks]

    def forward(k, r):
        fwd[k][r] = push(ggath.at[k, r], gfwd.at[k, r], fw_s.at[k, r], fw_r.at[k, r], mate)

    for k in ks:
        own = rs_next(k, zbits, *state[k], rt_out, rt_in, rt_s, rt_r)
        ggath[k, 0] = own.astype(BF16)
        gather_send(k, 0, zbits, ggath, gg_s, gg_r, waits[k])
        forward(k, 0)
    for j in reversed(range(1, zbits)):
        for k in ks:
            gather(waits[k], k, j, ggath, gg_s, gg_r, forward)
    node_state = []
    scale = 1.0 / math.sqrt(total)

    def node_send(k, i, value):
        j = (i + k) % nbits
        wg_out[k, i] = value.astype(BF16)
        return push(wg_out.at[k, i], wg_in.at[k, i], wg_s.at[k, i], wg_r.at[k, i], n_peer(j))

    for k in ks:
        gather(waits[k], k, 0, ggath, gg_s, gg_r, forward)
        acc = jnp.zeros((fd, hc), F32)
        for r in range(zs):
            acc = acc + nn(x_pair[r, 0:fd, :], ggath[k, r])
        for r in range(zs):
            fwd[k][r].wait_recv()
            acc = acc + nn(x_send[r], gfwd[k, r])
        node_state.append(node_send(k, 0, acc))
    for r in range(zs):
        for parity, buf in ((core, ggath), (1 - core, gfwd)):
            total_rows = nt(weight[:, hs(0)], buf[0, r])
            for k in range(1, CHUNKS):
                total_rows = total_rows + nt(weight[:, hs(k)], buf[k, r])
            grad_feat[:, pl.ds(rows_of(r, parity), tr)] = total_rows.astype(BF16)
    for i in range(1, nbits + 1):
        for k in ks:
            node_state[k].wait_recv()
            value = wg_out[k, i - 1].astype(F32) + wg_in[k, i - 1].astype(F32)
            if i < nbits:
                node_state[k] = node_send(k, i, value)
            else:
                weight_grad[:, hs(k)] = value * scale
    for copy in sent:
        copy.wait_send()


def body(node_features, weight, out_bias, edge_tiles, tile_column, tile_count, grad_hidden):
    fd, _, rows = node_features.shape
    blocks = lax.axis_size("feat")
    nodes = lax.axis_size("node")
    zs = blocks // 2
    nbits = nodes.bit_length() - 1
    tr = rows // blocks
    hw = weight.shape[1]
    hc = hw // CHUNKS
    slots = edge_tiles.shape[2]
    sizes = (zs, nodes, slots, tr, fd, hw, nodes * rows)
    vmem = pl.BlockSpec(memory_space=pltpu.VMEM)
    smem = pl.BlockSpec(memory_space=pltpu.SMEM)
    dma = pltpu.SemaphoreType.DMA
    c = CHUNKS
    scratch = [
        pltpu.VMEM((zs, fd, tr), BF16),
        pltpu.VMEM((zs, 2 * fd, tr), BF16),
        pltpu.VMEM((2 * fd, hw), BF16),
        pltpu.VMEM((tr, zs * tr), BF16),
        pltpu.VMEM((2 * tr, zs * tr), BF16),
        pltpu.VMEM((c, zs, tr, hc), BF16),
        pltpu.VMEM((c, zs, tr, hc), BF16),
        pltpu.VMEM((c, zs, tr, hc), BF16),
        pltpu.VMEM((c, tr, hc), F32),
        pltpu.VMEM((c, tr, hc), F32),
        pltpu.VMEM((c, 2 * tr, hc), BF16),
        pltpu.VMEM((c, zs, tr, hc), BF16),
        pltpu.VMEM((c, zs, tr, hc), BF16),
        pltpu.VMEM((c, zs, tr, hc), BF16),
        pltpu.VMEM((c, zs, tr, hc), BF16),
        pltpu.VMEM((c, nbits, fd, hc), BF16),
        pltpu.VMEM((c, nbits, fd, hc), BF16),
    ]
    for shape in ((3,), (c, zs), (c, zs), (c,), (c,), (c, zs), (c, zs), (c, zs), (c, nbits)):
        scratch += [dma(shape), dma(shape)]
    hidden, grad_feat, weight_grad = pl.pallas_call(
        functools.partial(kernel, sizes),
        out_shape=(
            jax.ShapeDtypeStruct((tr, hw), BF16),
            jax.ShapeDtypeStruct((fd, rows), BF16),
            jax.ShapeDtypeStruct((fd, hw), F32),
        ),
        in_specs=[smem, smem, vmem, vmem, vmem, vmem, vmem],
        out_specs=(vmem, vmem, vmem),
        scratch_shapes=scratch,
        compiler_params=pltpu.CompilerParams(
            collective_id=0, has_side_effects=True, vmem_limit_bytes=48 * 1024 * 1024
        ),
        name="sage",
    )(
        tile_column.reshape(slots),
        tile_count.reshape(1),
        node_features.reshape(fd, rows),
        weight,
        out_bias.reshape(1, hw),
        edge_tiles.reshape(slots, tr, tr),
        grad_hidden.reshape(tr, hw),
    )
    return (hidden[None], grad_feat[:, None, :], weight_grad)


def solution(mesh):
    return jax.shard_map(
        body,
        mesh=mesh,
        in_specs=(
            P("feat", "node", None),
            P("feat", None),
            P(),
            P("node", "feat", None, None, None),
            P("node", "feat", None),
            P("node", "feat"),
            P("node", "feat", None),
        ),
        out_specs=(P("node", "feat", None), P("feat", "node", None), P("feat", None)),
        check_vma=False,
    )
```

```python
import functools
import math

import jax
import jax.numpy as jnp
from jax import lax
from jax.experimental import pallas as pl
from jax.experimental.pallas import tpu as pltpu
from jax.sharding import PartitionSpec as P

MESH = pl.DeviceIdType.MESH
F32 = jnp.float32
BF16 = jnp.bfloat16
CHUNKS = 2
ROOT = math.sqrt(2.0 / math.pi)


def flip(index, bit):
    return index + bit * (1 - 2 * ((index // bit) % 2))


def flip_many(index, mask, steps):
    for j in range(steps):
        if (mask >> j) & 1:
            index = flip(index, 1 << j)
    return index


def tn(a, b):
    return lax.dot_general(a, b, (((0,), (0,)), ((), ())), preferred_element_type=F32)


def nt(a, b):
    return lax.dot_general(a, b, (((1,), (1,)), ((), ())), preferred_element_type=F32)


def nn(a, b):
    return lax.dot_general(a, b, (((1,), (0,)), ((), ())), preferred_element_type=F32)


def kernel(sizes, cols_hbm, count_hbm, feats, weight_hbm, bias_hbm, tiles_hbm, grad_hbm,
           hidden, grad_feat, weight_grad,
           cols, count, weight, bias, tiles, grad_hidden, in_s, xa_s, xb_s, xs_s, xs_r,
           x_send, x_pair, w_pair, a_send, a_pair,
           rs_out, rs_in, gath, part_out, part_in, sc_pair, rt_out, rt_in, ggath, gfwd,
           wg_in,
           ex_s, ex_r, rs_s, rs_r, ag_s, ag_r, p_s, p_r, s_s, s_r, rt_s, rt_r,
           gg_s, gg_r, fw_s, fw_r, wg_s, wg_r):
    zs, nodes, slots, tr, fd, hw, total = sizes
    zbits, nbits = zs.bit_length() - 1, nodes.bit_length() - 1
    hc = hw // CHUNKS
    feat_at = lax.axis_index("feat")
    node_at = lax.axis_index("node")
    core = feat_at % 2
    z = feat_at // 2
    mate = {"feat": z * 2 + 1 - core}

    zrel = [flip_many(z, r, zbits) for r in range(zs)]

    def z_peer(r):
        return {"feat": zrel[r] * 2 + core}

    def n_peer(n):
        return {"node": flip_many(node_at, n, nbits)}

    def push(src, dst, ss, rr, dev):
        copy = pltpu.make_async_remote_copy(
            src_ref=src, dst_ref=dst, send_sem=ss, recv_sem=rr,
            device_id=dev, device_id_type=MESH)
        copy.start()
        sent.append(copy)
        return copy

    sent = []
    far = list(reversed(range(1, zs)))
    barrier = pltpu.get_barrier_semaphore()
    peers = [mate] + [z_peer(r) for r in range(1, zs)] + [n_peer(n) for n in range(1, nodes)]
    for dev in peers:
        pl.semaphore_signal(barrier, inc=1, device_id=dev, device_id_type=MESH)

    def rows_of(r, parity):
        return pl.multiple_of((zrel[r] * 2 + parity) * tr, tr)

    def fetch(src, dst, sem):
        copy = pltpu.make_async_copy(src, dst, sem)
        copy.start()
        return copy

    loads = [fetch(src, dst, in_s.at[i]) for i, (src, dst) in enumerate((
        (cols_hbm, cols), (count_hbm, count), (tiles_hbm, tiles), (weight_hbm, weight),
        (bias_hbm, bias), (grad_hbm, grad_hidden)))]
    x_mine = [fetch(feats.at[:, pl.ds(rows_of(r, core), tr)],
                    x_pair.at[r, pl.ds(0, fd)], xa_s.at[r]) for r in range(zs)]
    x_other = [fetch(feats.at[:, pl.ds(rows_of(r, 1 - core), tr)],
                     x_send.at[r], xb_s.at[r]) for r in range(zs)]
    for i in range(4):
        loads[i].wait()
    w_pair[0:fd, :] = weight[...]

    degree = jnp.zeros((tr, 1), F32)
    live = count[0, 0]

    def listed(block):
        where = jnp.int32(0)
        alive = jnp.int32(0)
        for s in range(slots):
            hit = cols[0, 0, s] == block
            where = jnp.where(hit, s, where)
            alive = jnp.where(hit, jnp.where(s < live, 1, 0), alive)
        return tiles[where].astype(F32) * alive.astype(F32)

    for r in range(zs):
        other = listed(zrel[r] * 2 + 1 - core)
        a_send[:, r * tr:(r + 1) * tr] = other.astype(BF16)
        mine = listed(zrel[r] * 2 + core)
        a_pair[0:tr, r * tr:(r + 1) * tr] = mine.astype(BF16)
        degree = degree + jnp.sum(mine + other, axis=1, keepdims=True)
    pl.semaphore_wait(barrier, len(peers))
    ex_w = push(weight_hbm, w_pair.at[pl.ds(fd, fd)], ex_s.at[1], ex_r.at[1], mate)
    ex_x = {r: push(feats.at[:, pl.ds(rows_of(r, 1 - core), tr)],
                    x_pair.at[r, pl.ds(fd, fd)], xs_s.at[r], xs_r.at[r], mate)
            for r in far + [0]}
    ex_a = push(a_send, a_pair.at[pl.ds(tr, tr)], ex_s.at[2], ex_r.at[2], mate)
    row_scale = lax.rsqrt(degree)
    for i in range(4, 6):
        loads[i].wait()
    for copy in x_mine + x_other:
        copy.wait()
    ex_w.wait_recv()

    def hs(k):
        return slice(k * hc, (k + 1) * hc)

    ks = range(CHUNKS)

    def send_terms(k, make, out, into, ss, rr):
        copies = []
        for r in far:
            out[k, r] = make(k, r).astype(BF16)
            copies.append(push(out.at[k, r], into.at[k, r], ss.at[k, r], rr.at[k, r], z_peer(r)))
        return make(k, 0), copies

    def take_terms(k, kept, copies, into):
        for copy in copies:
            copy.wait_recv()
        for r in far:
            kept = kept + into[k, r].astype(F32)
        return kept.astype(BF16)

    def gather_send(k, buf, ss, rr):
        return {r: push(buf.at[k, 0], buf.at[k, r], ss.at[k, r], rr.at[k, r], z_peer(r))
                for r in far}

    def project(k, r):
        if k == 0:
            ex_x[r].wait_recv()
        return tn(x_pair[r], w_pair[:, hs(k)])

    state = [send_terms(k, project, rs_out, rs_in, rs_s, rs_r) for k in ks]
    waits = []
    for k in ks:
        gath[k, 0] = take_terms(k, *state[k], rs_in)
        waits.append(gather_send(k, gath, ag_s, ag_r))
    ex_a.wait_recv()
    mine_sum, parts = [], []
    for k in ks:
        for r in far:
            waits[k][r].wait_recv()
        both = nn(a_pair[...], gath[k].reshape(zs * tr, hc))
        part_out[k] = both[tr:]
        parts.append(push(part_out.at[k], part_in.at[k], p_s.at[k], p_r.at[k], mate))
        mine_sum.append(both[:tr])
    scs = []
    for k in ks:
        parts[k].wait_recv()
        v = (mine_sum[k] + part_in[k]) * row_scale + bias[:, hs(k)]
        v2 = v * v
        t = jnp.tanh(ROOT * (v + 0.044715 * v2 * v))
        hidden[:, hs(k)] = (0.5 * v * (1.0 + t)).astype(BF16)
        slope = 0.5 * (1.0 + t) + 0.5 * v * (1.0 - t * t) * (ROOT * (1.0 + 3 * 0.044715 * v2))
        grad_pre = grad_hidden[:, hs(k)].astype(F32) * slope
        sc_pair[k, 0:tr] = (grad_pre * row_scale).astype(BF16)
        scs.append(push(sc_pair.at[k, pl.ds(0, tr)], sc_pair.at[k, pl.ds(tr, tr)],
                        s_s.at[k], s_r.at[k], mate))

    def terms(k, r):
        if r == zs - 1:
            scs[k].wait_recv()
        return tn(a_pair[:, r * tr:(r + 1) * tr], sc_pair[k])

    state = [send_terms(k, terms, rt_out, rt_in, rt_s, rt_r) for k in ks]
    waits = []
    fwd = [dict() for _ in ks]

    def forward(k, r):
        fwd[k][r] = push(ggath.at[k, r], gfwd.at[k, r], fw_s.at[k, r], fw_r.at[k, r], mate)

    for k in ks:
        ggath[k, 0] = take_terms(k, *state[k], rt_in)
        waits.append(gather_send(k, ggath, gg_s, gg_r))
        forward(k, 0)
    node_state = []
    scale = 1.0 / math.sqrt(total)

    for k in ks:
        for r in range(1, zs):
            waits[k][r].wait_recv()
            forward(k, r)
        acc = jnp.zeros((fd, hc), F32)
        for r in range(zs):
            acc = acc + nn(x_pair[r, 0:fd, :], ggath[k, r])
        for r in range(zs):
            fwd[k][r].wait_recv()
            acc = acc + nn(x_send[r], gfwd[k, r])
        wg_in[k, 0] = acc.astype(BF16)
        node_state.append([push(wg_in.at[k, 0], wg_in.at[k, n], wg_s.at[k, n], wg_r.at[k, n],
                                n_peer(n)) for n in reversed(range(1, nodes))])
    for r in range(zs):
        for parity, buf in ((core, ggath), (1 - core, gfwd)):
            total_rows = nt(weight[:, hs(0)], buf[0, r])
            for k in range(1, CHUNKS):
                total_rows = total_rows + nt(weight[:, hs(k)], buf[k, r])
            grad_feat[:, pl.ds(rows_of(r, parity), tr)] = total_rows.astype(BF16)
    for k in ks:
        for copy in node_state[k]:
            copy.wait_recv()
        level = [wg_in[k, n].astype(F32) for n in range(nodes)]
        while len(level) > 1:
            level = [level[i] + level[i + 1] for i in range(0, len(level), 2)]
        weight_grad[:, hs(k)] = level[0] * scale
    for copy in sent:
        copy.wait_send()


def write_out(a, b, c, a_out, b_out, c_out, sems):
    pairs = ((a, a_out), (b, b_out), (c, c_out))
    copies = [pltpu.make_async_copy(x, y, sems.at[i]) for i, (x, y) in enumerate(pairs)]
    for copy in copies:
        copy.start()
    for copy in copies:
        copy.wait()


def body(node_features, weight, out_bias, edge_tiles, tile_column, tile_count, grad_hidden):
    fd, _, rows = node_features.shape
    blocks = lax.axis_size("feat")
    nodes = lax.axis_size("node")
    zs = blocks // 2
    tr = rows // blocks
    hw = weight.shape[1]
    hc = hw // CHUNKS
    slots = edge_tiles.shape[2]
    sizes = (zs, nodes, slots, tr, fd, hw, nodes * rows)
    vmem = pl.BlockSpec(memory_space=pltpu.VMEM)
    hbm = pl.BlockSpec(memory_space=pltpu.HBM)
    dma = pltpu.SemaphoreType.DMA
    c = CHUNKS
    scratch = [
        pltpu.SMEM((1, 1, slots), jnp.int32),
        pltpu.SMEM((1, 1), jnp.int32),
        pltpu.VMEM((fd, hw), BF16),
        pltpu.VMEM((1, hw), F32),
        pltpu.VMEM((slots, tr, tr), BF16),
        pltpu.VMEM((tr, hw), BF16),
        dma((6,)),
        dma((zs,)),
        dma((zs,)),
        dma((zs,)),
        dma((zs,)),
        pltpu.VMEM((zs, fd, tr), BF16),
        pltpu.VMEM((zs, 2 * fd, tr), BF16),
        pltpu.VMEM((2 * fd, hw), BF16),
        pltpu.VMEM((tr, zs * tr), BF16),
        pltpu.VMEM((2 * tr, zs * tr), BF16),
        pltpu.VMEM((c, zs, tr, hc), BF16),
        pltpu.VMEM((c, zs, tr, hc), BF16),
        pltpu.VMEM((c, zs, tr, hc), BF16),
        pltpu.VMEM((c, tr, hc), F32),
        pltpu.VMEM((c, tr, hc), F32),
        pltpu.VMEM((c, 2 * tr, hc), BF16),
        pltpu.VMEM((c, zs, tr, hc), BF16),
        pltpu.VMEM((c, zs, tr, hc), BF16),
        pltpu.VMEM((c, zs, tr, hc), BF16),
        pltpu.VMEM((c, zs, tr, hc), BF16),
        pltpu.VMEM((c, nodes, fd, hc), BF16),
    ]
    for shape in ((3,), (c, zs), (c, zs), (c,), (c,), (c, zs), (c, zs), (c, zs), (c, nodes)):
        scratch += [dma(shape), dma(shape)]
    hidden, grad_feat, weight_grad = pl.pallas_call(
        functools.partial(kernel, sizes),
        out_shape=(
            jax.ShapeDtypeStruct((tr, hw), BF16),
            jax.ShapeDtypeStruct((fd, rows), BF16),
            jax.ShapeDtypeStruct((fd, hw), F32),
        ),
        in_specs=[hbm] * 7,
        out_specs=(vmem, vmem, vmem),
        scratch_shapes=scratch,
        compiler_params=pltpu.CompilerParams(
            collective_id=0, has_side_effects=True, vmem_limit_bytes=63 * 1024 * 1024
        ),
        name="sage",
    )(
        tile_column,
        tile_count,
        node_features.reshape(fd, rows),
        weight,
        out_bias.reshape(1, hw),
        edge_tiles.reshape(slots, tr, tr),
        grad_hidden.reshape(tr, hw),
    )
    hidden, grad_feat, weight_grad = pl.pallas_call(
        write_out,
        out_shape=(
            jax.ShapeDtypeStruct((tr, hw), BF16),
            jax.ShapeDtypeStruct((fd, rows), BF16),
            jax.ShapeDtypeStruct((fd, hw), F32),
        ),
        in_specs=[vmem] * 3,
        out_specs=(hbm,) * 3,
        scratch_shapes=[dma((3,))],
        name="write_out",
    )(hidden, grad_feat, weight_grad)
    return (hidden[None], grad_feat[:, None, :], weight_grad)


def solution(mesh):
    return jax.shard_map(
        body,
        mesh=mesh,
        in_specs=(
            P("feat", "node", None),
            P("feat", None),
            P(),
            P("node", "feat", None, None, None),
            P("node", "feat", None),
            P("node", "feat"),
            P("node", "feat", None),
        ),
        out_specs=(P("node", "feat", None), P("feat", "node", None), P("feat", None)),
        check_vma=False,
    )
```
